32 devices in a mesh: dp: 2 (over x), expert: 16 (over z, y, core).
Axes of the slice: x: 2, y: 2, z: 4, core: 2. Of those that a mesh axis runs over, the one named last changes fastest.
Arguments:
- tokens: bfloat16 [2, 8192, 1024], P(None, ('dp', 'expert')), may hold values from -6 to 6
- cotangent: bfloat16 [2, 8192, 1024], P(None, ('dp', 'expert')), may hold values from -6 to 6
- segments: int32 [2, 32, 256], P(None, ('dp', 'expert')), may hold values from 0 to 3, never falling along the last dimension, each value on 1 to 128 neighbouring positions
- routes: int32 [2, 8192, 8], P(None, ('dp', 'expert')), may hold values from 0 to 15, all different within a row; in each aligned block of 256 rows (0 to 255, 256 to 511, ..., all dimensions but the last counted through in order) at most 144 rows name the same one
- norm_attn: bfloat16 [1024], P(('dp', 'expert')), may hold values from 0.5 to 1.5
- w_qkv: bfloat16 [1024, 2048], P(('dp', 'expert')), may hold values from -0.1875 to 0.1875
- w_attn_out: bfloat16 [1024, 1024], P(('dp', 'expert')), may hold values from -1.5 to 1.5
- norm_ffn: bfloat16 [1024], P(('dp', 'expert')), may hold values from 0.5 to 1.5
- w_router: bfloat16 [1024, 16], P(('dp', 'expert')), may hold values from -0.1875 to 0.1875
- w_expert_in: bfloat16 [16, 1024, 1024], P('expert', 'dp'), may hold values from -0.1875 to 0.1875
- w_expert_out: bfloat16 [16, 512, 1024], P('expert', None, 'dp'), may hold values from -0.5 to 0.5
Outputs:
- out_tokens: bfloat16 [2, 8192, 1024], P(None, ('dp', 'expert'))
- grad_tokens: bfloat16 [2, 8192, 1024], P(None, ('dp', 'expert'))
- grad_norm_attn: float32 [1024], P(('dp', 'expert'))
- grad_w_qkv: float32 [1024, 2048], P(('dp', 'expert'))
- grad_w_attn_out: float32 [1024, 1024], P(('dp', 'expert'))
- grad_norm_ffn: float32 [1024], P(('dp', 'expert'))
- grad_w_router: float32 [1024, 16], P(('dp', 'expert'))
- grad_w_expert_in: float32 [16, 1024, 1024], P('expert', 'dp')
- grad_w_expert_out: float32 [16, 512, 1024], P('expert', None, 'dp')
The draws below stay inside these ranges and needn't reach their ends.
Inputs may be any that keep to these rules, and one draw needn't show every extreme that they name: In each aligned block of 256 rows of routes (one device's tokens of one micro-batch) no expert is named by more than 144 rows; the 8 experts of a token differ. `segments`: within each pack the document ids never fall; a document has at most 128 tokens; tokens attend only within their document.
All inputs are finite; a program needn't handle non-finite values.
Results may differ from the reference program's by a relative error of at most 0.014.
The reference program's roundings to bfloat16 on the way count: a program that leaves them out, or rounds other values in their place, can miss the bound.
Values may be sent and summed in bfloat16 or wider, within the bound.
No kernel may reach another device: no remote copies, remote signals or barrier semaphores. Data moves between devices by JAX's collectives and lax.ppermute only.
A program may use at most 192 MiB of HBM per device.

```python
import math
import jax
import jax.numpy as jnp
import numpy as np
from jax import lax

D = 1024
HQ = 16
KV = 8
HD = 64
H = 512
TOPK = 8
PACK = 256
DOCS = 4
MB = 2
EXPERTS = 16
QKV = 2048
CAP = 144
TOKENS_MB = 8192
DEVICES = 32


def block_levels(own_key, extent, split, smallest, largest):
    def one(axis_at, shards_of):
        heights = jax.random.uniform(jax.random.fold_in(jax.random.fold_in(own_key, 6), axis_at), (shards_of,), jnp.float32, smallest / len(split), largest / len(split))
        return jnp.repeat(jnp.exp(heights), extent[axis_at] // shards_of).reshape((-1,) + (1,) * (len(extent) - axis_at - 1))

    level = one(*split[0])
    for cut in split[1:]:
        level = level * one(*cut)
    return level


def split_up(count, total, limit, slope):
    portions = [(1 << 20) // math.isqrt(standing ** slope) + 1 for standing in range(2, count + 1)]
    surplus, holding = total - limit - (count - 1), [1] * (count - 1)
    while surplus > 0:
        free = [i for i in range(count - 1) if holding[i] < limit]
        whole, remaining = sum([portions[i] for i in free]), surplus
        for i in free:
            addition = min(limit - holding[i], max(1, remaining * portions[i] // whole), surplus)
            holding[i] = holding[i] + addition
            surplus = surplus - addition
    return np.array([limit] + holding)


def ragged_sizes(key, count, total, limit, lean):
    if count == 2:
        one = jax.random.randint(key, (), max(1, total - limit), min(limit, total - 1) + 1)
        return jnp.stack([one, total - one])
    tallies = jnp.asarray(split_up(count, total, limit, lean), jnp.int32)
    twos = (count - 1) // 2
    donor, taker = tallies[1:1 + 2 * twos:2], tallies[2:2 + 2 * twos:2]
    slack = jnp.minimum(donor - 1, limit - taker)
    moved = jax.random.randint(jax.random.fold_in(key, 1), (twos,), 0, 1 << 20) % (slack + 1)
    tallies = tallies.at[1:1 + 2 * twos:2].set(donor - moved).at[2:2 + 2 * twos:2].set(taker + moved)
    return tallies[jax.random.permutation(jax.random.fold_in(key, 2), count)]


def assign_block(rng, own, number, rows, count, top, most, lean):
    ranking = jax.random.permutation(rng, count)
    crowded, common = load_shares(count, rows * top, most, lean, True), load_shares(count, rows * top, most, lean, False)
    places = jnp.arange(count)

    def named(tallies, rotation):
        used = int((tallies > 0).sum())
        fixed = max(1, used // 4)
        moved = fixed + (places - fixed + rotation * (used - fixed)) % max(1, count - fixed)
        return jnp.zeros((count,), jnp.int32).at[ranking[jnp.where(places < fixed, places, moved)]].set(jnp.asarray(tallies, jnp.int32))

    tallies = jnp.where(number % 4 == 0, named(crowded, number // 4), named(common, number - number // 4 - 1))
    mixed = jax.random.permutation(jax.random.fold_in(own, 3), count)
    source_of, sink = mixed[0:count // 2 * 2:2], mixed[1:count // 2 * 2:2]
    room = jnp.minimum(tallies[source_of] - 1, most - tallies[sink]) // 2
    room = jnp.where((source_of == ranking[0]) | (sink == ranking[0]) | (tallies[sink] == 0), 0, jnp.maximum(room, 0))
    moved = jax.random.randint(jax.random.fold_in(own, 4), (count // 2,), 0, 1 << 20) % (room + 1)
    tallies = tallies.at[source_of].add(-moved).at[sink].add(moved)
    labels = jnp.searchsorted(jnp.cumsum(tallies), jnp.arange(rows * top), side="right").astype(jnp.int32)
    table = labels.reshape(top, rows).T
    table = table[jax.random.permutation(jax.random.fold_in(own, 1), rows)]
    rotation = jax.random.randint(jax.random.fold_in(own, 2), (rows, 1), 0, top)
    return jnp.take_along_axis(table, (jnp.arange(top)[None, :] + rotation) % top, axis=1)


def load_shares(amount, total, limit, lean, full):
    weights = [(1 << 20) // math.isqrt(rank ** lean) + 1 for rank in range(1, amount + 1)]
    largest = limit if full else min(limit, max(-(-total // amount), total * weights[0] // sum(weights)))
    least = 1 if total - largest >= amount - 1 else 0
    holding, rest = [largest] + [least] * (amount - 1), total - largest - least * (amount - 1)
    while rest > 0:
        movable = [i for i in range(1, amount) if holding[i] < largest] or [i for i in range(1, amount) if holding[i] < limit]
        pool, remaining = sum([weights[i] for i in movable]), rest
        for i in movable:
            addition = min(limit - holding[i], max(1, remaining * weights[i] // pool), rest)
            holding[i] = holding[i] + addition
            rest = rest - addition
    return np.array(holding)


def noise(rng, dims, spread, most, pieces=(), kind=jnp.bfloat16):
    result = jax.random.normal(rng, dims, jnp.float32) * spread
    if len(pieces) > 0:
        result = block_levels(rng, dims, pieces, -0.22, 0.18) * result
    return jnp.clip(result, min=-most, max=most).astype(kind)


def setup_inputs(seed: int = 0) -> dict:
    seeds = jax.random.split(jax.random.key(seed), 12)
    tokens = noise(seeds[0], (MB, TOKENS_MB, D), 1.0, 6.0, ((1, 32),))
    cotangent = noise(seeds[1], (MB, TOKENS_MB, D), 1.0, 6.0, ((1, 32),))
    segments = jax.vmap(lambda own: jnp.searchsorted(jnp.cumsum(ragged_sizes(own, DOCS, PACK, PACK // 2, 2)), jnp.arange(PACK), side="right"))(jax.random.split(seeds[2], MB * DEVICES)).reshape((MB, DEVICES, PACK)).astype(jnp.int32)
    routes_keys = jax.random.split(jax.random.fold_in(seeds[3], 1), MB * TOKENS_MB // PACK)
    routes_turns = jax.random.permutation(jax.random.fold_in(seeds[3], 3), MB * TOKENS_MB // PACK)
    routes = jax.vmap(lambda own, number: assign_block(jax.random.fold_in(seeds[3], 2), own, number, PACK, EXPERTS, TOPK, CAP, 1))(routes_keys, routes_turns).reshape((MB, TOKENS_MB, TOPK))
    norm_attn = jnp.clip(1.0 + 0.1 * jax.random.normal(seeds[4], (D,), jnp.float32), 0.5, 1.5).astype(jnp.bfloat16)
    w_qkv = noise(seeds[5], (D, QKV), D ** -0.5, 0.1875, ((0, 32),))
    w_attn_out = noise(seeds[6], (HQ * HD, D), (HQ * HD // 64) ** -0.5, 1.5, ((0, 32),))
    norm_ffn = jnp.clip(1.0 + 0.1 * jax.random.normal(seeds[7], (D,), jnp.float32), 0.5, 1.5).astype(jnp.bfloat16)
    w_router = noise(seeds[8], (D, EXPERTS), D ** -0.5, 0.1875, ((0, 32),))
    w_expert_in = noise(seeds[9], (EXPERTS, D, 2 * H), D ** -0.5, 0.1875, ((0, 16), (1, 2)))
    w_expert_out = noise(seeds[10], (EXPERTS, H, D), (H // 4) ** -0.5, 0.5, ((0, 16), (2, 2)))
    return dict(tokens=tokens, cotangent=cotangent, segments=segments, routes=routes, norm_attn=norm_attn, w_qkv=w_qkv, w_attn_out=w_attn_out, norm_ffn=norm_ffn, w_router=w_router, w_expert_in=w_expert_in, w_expert_out=w_expert_out)


@jax.custom_vjp
def low(v):
    return lax.optimization_barrier(v.astype(jnp.bfloat16)).astype(jnp.float32)

@jax.custom_vjp
def low_back(v):
    return v

def low_keep(v):
    return (low(v), None)

def low_pass(kept, grad):
    return (grad,)

def back_keep(v):
    return (v, None)

def back_low(kept, grad):
    return (low(grad),)
low.defvjp(low_keep, low_pass)
low_back.defvjp(back_keep, back_low)
eps_norm = 1e-06
masked_score = -1e+30

def rms_scale(values_in, gain_row):
    return values_in * lax.rsqrt(lax.optimization_barrier(jnp.mean(values_in * values_in, axis=-1, keepdims=True)) + eps_norm) * gain_row

def rope_angles(segment_row, head_size):
    length = segment_row.shape[0]
    position_index = jnp.arange(length, dtype=jnp.int32)
    change = jnp.concatenate([jnp.ones((1,), dtype=bool), segment_row[1:] != segment_row[:-1]])
    doc_start = lax.cummax(jnp.where(change, position_index, 0).astype(jnp.int32), axis=0)
    doc_place = (position_index - doc_start).astype(jnp.float32)
    frequency = 10000.0 ** (-jnp.arange(head_size // 2, dtype=jnp.float32) * (2.0 / head_size))
    angles = doc_place[:, None] * frequency[None, :]
    return (jnp.cos(angles), jnp.sin(angles), position_index)

def rotate(vectors, cosine, sine_table):
    half_width = vectors.shape[-1] // 2
    first_half = vectors[..., :half_width]
    second_half = vectors[..., half_width:]
    return jnp.concatenate([first_half * cosine - second_half * sine_table, second_half * cosine + first_half * sine_table], axis=-1)

def pack_attention(pack_item):
    projected, segment_row = pack_item
    cosine, sine_table, position_index = rope_angles(segment_row, HD)
    query = projected[:, :HQ * HD].reshape(PACK, HQ, HD).transpose(1, 0, 2)
    key_rows = projected[:, HQ * HD:(HQ + KV) * HD].reshape(PACK, KV, HD).transpose(1, 0, 2)
    value_rows = projected[:, (HQ + KV) * HD:].reshape(PACK, KV, HD).transpose(1, 0, 2)
    query = low(rotate(query, cosine, sine_table)).reshape(KV, HQ // KV, PACK, HD)
    key_rows = low(rotate(key_rows, cosine, sine_table))
    value_rows = low(value_rows)
    scores = jnp.einsum('kgqd,ksd->kgqs', query, key_rows, precision=lax.Precision.HIGHEST)
    scores = low_back(scores * HD ** (-0.5))
    allowed = (segment_row[:, None] == segment_row[None, :]) & (position_index[:, None] >= position_index[None, :])
    scores = jnp.where(allowed, scores, masked_score)
    top_score = lax.optimization_barrier(jnp.max(scores, axis=-1, keepdims=True))
    exponent = jnp.exp(scores - top_score)
    probabilities = low(exponent / lax.optimization_barrier(jnp.sum(exponent, axis=-1, keepdims=True)))
    attended = jnp.einsum('kgqs,ksd->kgqd', probabilities, value_rows, precision=lax.Precision.HIGHEST)
    return attended.reshape(HQ, PACK, HD).transpose(1, 0, 2).reshape(PACK, HQ * HD)

def block_forward(weights, rows_in, segment_rows, route_rows):
    gain_attn, qkv_weight, out_weight, gain_ffn, router_weight, expert_in_weight, expert_out_weight = weights
    row_count = rows_in.shape[0]
    normed = low(rms_scale(rows_in, gain_attn))
    projected = low_back(jnp.dot(normed, qkv_weight, precision=lax.Precision.HIGHEST))
    attended = lax.map(jax.checkpoint(pack_attention), (projected.reshape(row_count // PACK, PACK, QKV), segment_rows))
    attended = low_back(low(attended.reshape(row_count, HQ * HD)))
    residual = rows_in + low_back(jnp.dot(attended, out_weight, precision=lax.Precision.HIGHEST))
    ffn_in = low(rms_scale(residual, gain_ffn))
    logits = low_back(jnp.dot(ffn_in, router_weight, precision=lax.Precision.HIGHEST))
    chosen = jnp.take_along_axis(logits, route_rows, axis=1)
    gate = jax.nn.softmax(chosen, axis=-1)
    onehot = (route_rows[:, :, None] == jnp.arange(EXPERTS, dtype=jnp.int32)[None, None, :]).astype(jnp.float32)
    gate_share = jnp.einsum('tk,tke->et', gate, onehot, precision=lax.Precision.HIGHEST)

    def expert_step(running, expert_item):
        weight_in, weight_out, column = expert_item
        expert_in = low_back(ffn_in)
        gate_up = low_back(jnp.dot(expert_in, weight_in, precision=lax.Precision.HIGHEST))
        gated = jax.nn.silu(gate_up[:, :H]) * gate_up[:, H:]
        expert_out = low_back(low(jnp.dot(low(gated), weight_out, precision=lax.Precision.HIGHEST)))
        return (running + column[:, None] * expert_out, None)
    mixture, _ = lax.scan(jax.checkpoint(expert_step), jnp.zeros_like(rows_in), (expert_in_weight, expert_out_weight, gate_share))
    return residual + mixture

def reference(tokens, cotangent, segments, routes, norm_attn, w_qkv, w_attn_out, norm_ffn, w_router, w_expert_in, w_expert_out):
    pack_count = MB * TOKENS_MB // PACK
    per_block = math.gcd(pack_count, max(1, 4096 // PACK))
    block_count = pack_count // per_block
    rows_all = tokens.astype(jnp.float32).reshape(block_count, per_block * PACK, D)
    segment_blocks = segments.reshape(block_count, per_block, PACK)
    route_blocks = routes.reshape(block_count, per_block * PACK, TOPK)
    weight_list = (norm_attn.astype(jnp.float32), w_qkv.astype(jnp.float32), w_attn_out.astype(jnp.float32), norm_ffn.astype(jnp.float32), w_router.astype(jnp.float32), w_expert_in.astype(jnp.float32), w_expert_out.astype(jnp.float32))

    def forward(rows_in, gain_attn, qkv_weight, out_weight, gain_ffn, router_weight, expert_in_weight, expert_out_weight):
        weights = (gain_attn, qkv_weight, out_weight, gain_ffn, router_weight, expert_in_weight, expert_out_weight)

        def one_block(block_item):
            block_rows, block_segments, block_routes = block_item
            return block_forward(weights, block_rows, block_segments, block_routes)
        return lax.map(jax.checkpoint(one_block), (rows_in, segment_blocks, route_blocks))
    output_rows, pullback = jax.vjp(forward, rows_all, *weight_list)
    grads = pullback(cotangent.astype(jnp.float32).reshape(rows_all.shape))
    return (output_rows.reshape(MB, TOKENS_MB, D).astype(jnp.bfloat16), grads[0].reshape(MB, TOKENS_MB, D).astype(jnp.bfloat16), grads[1], grads[2], grads[3], grads[4], grads[5], grads[6], grads[7])
```

```python
import jax
import jax.numpy as jnp
from jax import lax
from jax.sharding import PartitionSpec as P

HQ = 16
KV = 8
HD = 64
Z = 4
C = 2

eps_norm = 1e-06
masked_score = -1e30
BF = jnp.bfloat16
F32 = jnp.float32


def rms_scale(values_in, gain_row):
    return (
        values_in
        * lax.rsqrt(jnp.mean(values_in * values_in, axis=-1, keepdims=True) + eps_norm)
        * gain_row
    )


def rope_angles(segment_row, head_size):
    length = segment_row.shape[0]
    position_index = jnp.arange(length, dtype=jnp.int32)
    doc_start = jnp.sum(
        (segment_row[None, :] < segment_row[:, None]).astype(jnp.int32), axis=1
    )
    doc_place = (position_index - doc_start).astype(F32)
    frequency = 10000.0 ** (-jnp.arange(head_size // 2, dtype=F32) * (2.0 / head_size))
    angles = doc_place[:, None] * frequency[None, :]
    return (jnp.cos(angles), jnp.sin(angles), position_index)


def rotate(vectors, cosine, sine_table):
    half_width = vectors.shape[-1] // 2
    first_half = vectors[..., :half_width]
    second_half = vectors[..., half_width:]
    return jnp.concatenate(
        [
            first_half * cosine - second_half * sine_table,
            second_half * cosine + first_half * sine_table,
        ],
        axis=-1,
    )


def masked_scores(query_low, keys_low, allowed, score_scale):
    scores = (
        jnp.einsum("kgqd,ksd->kgqs", query_low, keys_low, preferred_element_type=F32)
        * score_scale
    )
    return jnp.where(allowed, scores, masked_score)


def attend_forward(query_low, keys_low, values_low, allowed, score_scale):
    scores = masked_scores(query_low, keys_low, allowed, score_scale)
    top_score = jnp.max(scores, axis=-1, keepdims=True)
    exponent = jnp.exp(scores - top_score)
    row_total = jnp.sum(exponent, axis=-1, keepdims=True)
    probabilities = (exponent / row_total).astype(BF)
    attended = jnp.einsum("kgqs,ksd->kgqd", probabilities, values_low, preferred_element_type=F32)
    return (attended, top_score + jnp.log(row_total))


def attend_backward(query_low, keys_low, values_low, allowed, score_scale, logsum, grad_heads):
    scores = masked_scores(query_low, keys_low, allowed, score_scale)
    probabilities = jnp.exp(scores - logsum)
    grad_probs = jnp.einsum("kgqd,ksd->kgqs", grad_heads, values_low, preferred_element_type=F32)
    inner_sum = jnp.sum(probabilities * grad_probs, axis=-1, keepdims=True)
    grad_scores = (probabilities * (grad_probs - inner_sum)).astype(BF)
    grad_query = (
        jnp.einsum("kgqs,ksd->kgqd", grad_scores, keys_low, preferred_element_type=F32)
        * score_scale
    )
    grad_keys = (
        jnp.einsum("kgqs,kgqd->ksd", grad_scores, query_low, preferred_element_type=F32)
        * score_scale
    )
    grad_values = jnp.einsum(
        "kgqs,kgqd->ksd", probabilities.astype(BF), grad_heads, preferred_element_type=F32
    )
    return (grad_query, grad_keys, grad_values)


class Ring:
    def __init__(self):
        self.groups = lax.axis_size("expert")
        self.dp = lax.axis_size("dp")
        self.rows = self.groups // (Z * C)
        here = lax.axis_index("expert")
        self.x = lax.axis_index("dp")
        self.z = here // (self.rows * C)
        self.y = (here // C) % self.rows
        self.c = here % C

    def move(self, value, dz, dy, dc):
        pairs = []
        for place in range(self.groups):
            z, y, c = place // (self.rows * C), (place // C) % self.rows, place % C
            pairs.append(
                (
                    place,
                    ((z + dz) % Z) * self.rows * C + ((y + dy) % self.rows) * C + ((c + dc) % C),
                )
            )
        return lax.ppermute(value, "expert", pairs)

    def move_dp(self, value, shift):
        return lax.ppermute(value, "dp", [(i, (i + shift) % self.dp) for i in range(self.dp)])

    def gather(self, value):
        along_z = [value] + [self.move(value, s, 0, 0) for s in range(1, Z)]
        near = []
        for s in range(Z):
            near += [along_z[s]] + [self.move(along_z[s], 0, t, 0) for t in range(1, self.rows)]
        return near + [self.move(piece, 0, 0, 1) for piece in near]

    def relative(self):
        order = jnp.arange(self.groups, dtype=jnp.int32)
        u = order // (Z * self.rows)
        s = (order // self.rows) % Z
        t = order % self.rows
        source = (
            ((self.z - s) % Z) * (self.rows * C)
            + ((self.y - t) % self.rows) * C
            + ((self.c + u) % C)
        )
        return (source[:, None] == order[None, :]).astype(F32)

    def scatter_sum(self, blocks):
        half = Z * self.rows
        total = None
        for s in list(range(1, Z)) + [0]:
            part = None
            for t in list(range(1, self.rows)) + [0]:
                at = s * self.rows + t
                block = blocks[at] + self.move(blocks[half + at].astype(BF), 0, 0, 1).astype(F32)
                if t:
                    block = self.move(block.astype(BF), 0, -t, 0).astype(F32)
                part = block if part is None else part + block
            if s:
                part = self.move(part.astype(BF), -s, 0, 0).astype(F32)
            total = part if total is None else total + part
        return total

    def stage(self, value, coord, count, mover):
        total = lax.dynamic_index_in_dim(value, coord, 0, keepdims=False)
        for s in range(1, count):
            block = lax.dynamic_index_in_dim(value, (coord + s) % count, 0, keepdims=False)
            total = total + mover(block.astype(BF), s).astype(F32)
        return total

    def dense_sum(self, grad, y_first):
        width = grad.shape[1]
        rows = grad.shape[0] // (self.dp * self.groups)
        value = grad.reshape(self.dp, Z, self.rows, C, rows, width)
        value = jnp.moveaxis(value, 3, 0)
        value = self.stage(value, self.c, C, lambda v, s: self.move(v, 0, 0, s))

        def over_x(v):
            return self.stage(v, self.x, self.dp, self.move_dp)

        def over_y(v):
            return self.stage(v, self.y, self.rows, lambda b, s: self.move(b, 0, s, 0))

        if y_first:
            value = over_x(over_y(jnp.moveaxis(value, 2, 0)))
        else:
            value = over_y(jnp.moveaxis(over_x(value), 1, 0))
        return self.stage(value, self.z, Z, lambda v, s: self.move(v, s, 0, 0))


def on_device(
    tokens,
    cotangent,
    segments,
    routes,
    norm_attn,
    w_qkv,
    w_attn_out,
    norm_ffn,
    w_router,
    w_expert_in,
    w_expert_out,
):
    micro_count, pack_rows, model_width = tokens.shape
    ring = Ring()
    groups = ring.groups
    expert_count = w_expert_in.shape[0] * groups
    assert expert_count == groups
    top_count = routes.shape[2]
    capacity = pack_rows * top_count * 9 // (8 * expert_count)
    hidden = w_expert_out.shape[1]
    q_width = HQ * HD
    kv_width = KV * HD
    score_scale = HD ** (-0.5)
    expert_range = jnp.arange(expert_count, dtype=jnp.int32)
    micro = range(micro_count)
    both = ("dp", "expert")

    small = jnp.concatenate(
        [w_router, norm_attn[:, None], norm_ffn[:, None]], axis=1
    )
    small_all = lax.all_gather(small, both, axis=0, tiled=True)
    router_weight = small_all[:, :expert_count]
    gain_one = small_all[:, expert_count].astype(F32)
    gain_two = small_all[:, expert_count + 1].astype(F32)
    qkv_weight = lax.all_gather(w_qkv, both, axis=0, tiled=True)
    out_weight = lax.all_gather(w_attn_out, both, axis=0, tiled=True)
    expert_in_weight = lax.all_gather(w_expert_in[0], "dp", axis=0, tiled=True)
    expert_out_weight = lax.all_gather(w_expert_out[0], "dp", axis=1, tiled=True)

    relative = ring.relative()
    dense_mask = jnp.any(routes[..., None] == expert_range, axis=2)
    mask_sent = jnp.transpose(dense_mask.astype(F32), (2, 0, 1))
    mask_got = lax.all_to_all(mask_sent, "expert", split_axis=0, concat_axis=0, tiled=True)
    mask_rel = jnp.einsum("re,emt->mrt", relative, mask_got, precision=lax.Precision.HIGHEST)
    upper = jnp.triu(jnp.ones((pack_rows, pack_rows), BF))
    slots = (
        jnp.einsum("mrt,ts->mrs", mask_rel.astype(BF), upper, preferred_element_type=F32) - 1.0
    )
    slot_range = jnp.arange(capacity, dtype=jnp.int32)
    picks = [
        (slots[m][:, None, :].astype(jnp.int32) == slot_range[None, :, None])
        & (mask_rel[m][:, None, :] > 0.5)
        for m in micro
    ]

    dy_pieces = [ring.gather(cotangent[m]) for m in micro]

    saved = []
    for m in micro:
        rows_in = tokens[m].astype(F32)
        segment_row = segments[m, 0]
        cosine, sine_table, position_index = rope_angles(segment_row, HD)
        allowed = (segment_row[:, None] == segment_row[None, :]) & (
            position_index[:, None] >= position_index[None, :]
        )
        normed_low = rms_scale(rows_in, gain_one).astype(BF)
        projected = jnp.dot(normed_low, qkv_weight, preferred_element_type=F32)
        query = rotate(
            projected[:, :q_width].reshape(pack_rows, HQ, HD).transpose(1, 0, 2), cosine, sine_table
        )
        key_rows = rotate(
            projected[:, q_width : q_width + kv_width]
            .reshape(pack_rows, KV, HD)
            .transpose(1, 0, 2),
            cosine,
            sine_table,
        )
        value_rows = (
            projected[:, q_width + kv_width :].reshape(pack_rows, KV, HD).transpose(1, 0, 2)
        )
        query_low = query.astype(BF).reshape(KV, HQ // KV, pack_rows, HD)
        keys_low = key_rows.astype(BF)
        values_low = value_rows.astype(BF)
        attended, logsum = attend_forward(query_low, keys_low, values_low, allowed, score_scale)
        attended_low = (
            attended.reshape(HQ, pack_rows, HD)
            .transpose(1, 0, 2)
            .reshape(pack_rows, q_width)
            .astype(BF)
        )
        residual = rows_in + jnp.dot(attended_low, out_weight, preferred_element_type=F32)
        ffn_in = rms_scale(residual, gain_two).astype(BF)
        x_pieces = ring.gather(ffn_in)
        logits = jnp.dot(ffn_in, router_weight, preferred_element_type=F32)
        chosen = jnp.where(dense_mask[m], logits, -jnp.inf)
        top_logit = jnp.max(chosen, axis=-1, keepdims=True)
        powers = jnp.where(dense_mask[m], jnp.exp(chosen - top_logit), 0.0)
        gate = powers / jnp.sum(powers, axis=-1, keepdims=True)
        gate_got = lax.all_to_all(gate.T, "expert", split_axis=0, concat_axis=0, tiled=True)
        saved.append(
            dict(
                rows_in=rows_in,
                cosine=cosine,
                sine_table=sine_table,
                allowed=allowed,
                normed_low=normed_low,
                query_low=query_low,
                keys_low=keys_low,
                values_low=values_low,
                logsum=logsum,
                attended_low=attended_low,
                residual=residual,
                ffn_in=ffn_in,
                x_pieces=x_pieces,
                gate=gate,
                gate_got=gate_got,
            )
        )

    acc_expert_in = 0.0
    acc_expert_out = 0.0
    for m in micro:
        keep = saved[m]
        pick_low = picks[m].astype(BF)
        gate_rel = jnp.dot(relative, keep["gate_got"], precision=lax.Precision.HIGHEST)
        gate_slot = jnp.sum(jnp.where(picks[m], gate_rel[:, None, :], 0.0), axis=2)
        x_slot = jnp.concatenate(
            [
                jnp.dot(pick_low[r], keep["x_pieces"][r], preferred_element_type=F32).astype(BF)
                for r in range(groups)
            ]
        )
        dy_slot = jnp.concatenate(
            [
                jnp.dot(pick_low[r], dy_pieces[m][r], preferred_element_type=F32).astype(BF)
                for r in range(groups)
            ]
        )
        gate_up = jnp.dot(x_slot, expert_in_weight, preferred_element_type=F32)
        gate_part = gate_up[:, :hidden]
        up_part = gate_up[:, hidden:]
        sigmoid_gate = jax.nn.sigmoid(gate_part)
        activated = gate_part * sigmoid_gate
        product = (activated * up_part).astype(BF)
        result = jnp.dot(product, expert_out_weight, preferred_element_type=F32).astype(BF)
        dy_wide = dy_slot.astype(F32)
        grad_gate_slot = jnp.sum(dy_wide * result.astype(F32), axis=1).reshape(groups, capacity)
        grad_result = (gate_slot.reshape(-1, 1) * dy_wide).astype(BF)
        grad_product = jnp.einsum(
            "sd,fd->sf", grad_result, expert_out_weight, preferred_element_type=F32
        )
        grad_gate_part = (
            grad_product * up_part * sigmoid_gate * (1.0 + gate_part * (1.0 - sigmoid_gate))
        )
        grad_gate_up = jnp.concatenate(
            [grad_gate_part, grad_product * activated], axis=-1
        ).astype(BF)
        grad_slot = jnp.einsum(
            "sf,df->sd", grad_gate_up, expert_in_weight, preferred_element_type=F32
        ).astype(BF)
        acc_expert_out = acc_expert_out + jnp.einsum(
            "sf,sd->fd", product, grad_result, preferred_element_type=F32
        )
        acc_expert_in = acc_expert_in + jnp.einsum(
            "sd,sf->df", x_slot, grad_gate_up, preferred_element_type=F32
        )
        grad_gate_rel = jnp.sum(jnp.where(picks[m], grad_gate_slot[:, :, None], 0.0), axis=1)
        grad_gate_abs = jnp.einsum(
            "re,rt->et", relative, grad_gate_rel, precision=lax.Precision.HIGHEST
        )
        keep["grad_gate"] = lax.all_to_all(
            grad_gate_abs, "expert", split_axis=0, concat_axis=0, tiled=True
        ).T

        def back(rows, r):
            return jnp.einsum(
                "jt,jd->td",
                pick_low[r],
                rows[r * capacity : (r + 1) * capacity],
                preferred_element_type=F32,
            )

        keep["grad_ffn"] = ring.scatter_sum([back(grad_slot, r) for r in range(groups)])
        keep["mixture"] = ring.scatter_sum(
            [gate_rel[r][:, None] * back(result, r) for r in range(groups)]
        )

    outputs = []
    input_grads = []
    acc_gain_attn = 0.0
    acc_gain_ffn = 0.0
    acc_router = 0.0
    acc_attn_out = 0.0
    acc_qkv = 0.0
    for m in micro:
        keep = saved[m]
        residual = keep["residual"]
        rows_in = keep["rows_in"]
        gate = keep["gate"]
        outputs.append((residual + keep["mixture"]).astype(BF))
        grad_out = cotangent[m].astype(F32)
        grad_gate = keep["grad_gate"]
        grad_logits = (
            gate * (grad_gate - jnp.sum(gate * grad_gate, axis=-1, keepdims=True))
        ).astype(BF)
        grad_ffn = keep["grad_ffn"] + jnp.einsum(
            "te,de->td", grad_logits, router_weight, preferred_element_type=F32
        )
        acc_router = acc_router + jnp.einsum(
            "td,te->de", keep["ffn_in"], grad_logits, preferred_element_type=F32
        )
        _, second_pull = jax.vjp(rms_scale, residual, gain_two)
        grad_residual, grad_gain_two = second_pull(grad_ffn)
        grad_residual = grad_residual + grad_out
        acc_gain_ffn = acc_gain_ffn + grad_gain_two
        grad_residual_low = grad_residual.astype(BF)
        grad_attended = jnp.einsum(
            "td,qd->tq", grad_residual_low, out_weight, preferred_element_type=F32
        ).astype(BF)
        acc_attn_out = acc_attn_out + jnp.einsum(
            "tq,td->qd", keep["attended_low"], grad_residual_low, preferred_element_type=F32
        )
        grad_heads = (
            grad_attended.reshape(pack_rows, HQ, HD)
            .transpose(1, 0, 2)
            .reshape(KV, HQ // KV, pack_rows, HD)
        )
        grad_query, grad_keys, grad_values = attend_backward(
            keep["query_low"],
            keep["keys_low"],
            keep["values_low"],
            keep["allowed"],
            score_scale,
            keep["logsum"],
            grad_heads,
        )
        cosine, sine_table = keep["cosine"], keep["sine_table"]
        grad_query = rotate(grad_query.reshape(HQ, pack_rows, HD), cosine, -sine_table)
        grad_keys = rotate(grad_keys, cosine, -sine_table)
        grad_projected = jnp.concatenate(
            [
                grad_query.transpose(1, 0, 2).reshape(pack_rows, q_width),
                grad_keys.transpose(1, 0, 2).reshape(pack_rows, kv_width),
                grad_values.transpose(1, 0, 2).reshape(pack_rows, kv_width),
            ],
            axis=1,
        ).astype(BF)
        grad_normed = jnp.einsum(
            "tp,dp->td", grad_projected, qkv_weight, preferred_element_type=F32
        )
        acc_qkv = acc_qkv + jnp.einsum(
            "td,tp->dp", keep["normed_low"], grad_projected, preferred_element_type=F32
        )
        _, first_pull = jax.vjp(rms_scale, rows_in, gain_one)
        grad_rows, grad_gain_one = first_pull(grad_normed)
        acc_gain_attn = acc_gain_attn + grad_gain_one
        input_grads.append((grad_rows + grad_residual).astype(BF))

    sum_attn_out = ring.dense_sum(acc_attn_out, True)
    sum_qkv_left = ring.dense_sum(acc_qkv[:, :q_width], False)
    sum_qkv_right = ring.dense_sum(acc_qkv[:, q_width:], True)
    sum_small = ring.dense_sum(
        jnp.concatenate([acc_router, acc_gain_attn[:, None], acc_gain_ffn[:, None]], axis=1), False
    )
    in_rows = acc_expert_in.reshape(ring.dp, -1, 2 * hidden)
    sum_expert_in = ring.stage(in_rows, ring.x, ring.dp, ring.move_dp)
    out_cols = jnp.moveaxis(acc_expert_out.reshape(hidden, ring.dp, -1), 1, 0)
    sum_expert_out = ring.stage(out_cols, ring.x, ring.dp, ring.move_dp)
    return (
        jnp.stack(outputs),
        jnp.stack(input_grads),
        sum_small[:, expert_count],
        jnp.concatenate([sum_qkv_left, sum_qkv_right], axis=1),
        sum_attn_out,
        sum_small[:, expert_count + 1],
        sum_small[:, :expert_count],
        sum_expert_in[None],
        sum_expert_out[None],
    )


def solution(mesh):
    in_specs = (
        P(None, ("dp", "expert"), None),
        P(None, ("dp", "expert"), None),
        P(None, ("dp", "expert"), None),
        P(None, ("dp", "expert"), None),
        P(("dp", "expert")),
        P(("dp", "expert"), None),
        P(("dp", "expert"), None),
        P(("dp", "expert")),
        P(("dp", "expert"), None),
        P("expert", "dp", None),
        P("expert", None, "dp"),
    )
    out_specs = (
        P(None, ("dp", "expert"), None),
        P(None, ("dp", "expert"), None),
        P(("dp", "expert")),
        P(("dp", "expert"), None),
        P(("dp", "expert"), None),
        P(("dp", "expert")),
        P(("dp", "expert"), None),
        P("expert", "dp", None),
        P("expert", None, "dp"),
    )
    return jax.shard_map(
        on_device, mesh=mesh, in_specs=in_specs, out_specs=out_specs, check_vma=False
    )
```
